512 devices in a mesh: leaf: 64 (over y_lo, z, core), blk: 8 (over y_hi, x).
Axes of the slice: x: 4, y: 8 (y_hi: 2, y_lo: 4; y = y_hi * 4 + y_lo), z: 8, core: 2. Of those that a mesh axis runs over, the one named last changes fastest.
Arguments:
- leaf_rows: bfloat16 [128, 8, 512, 512], P('leaf', None, 'blk'), may hold values from -2 to 2
- leaf_weight: bfloat16 [128, 8, 512], P('leaf', None, 'blk'), may hold values from 0.25 to 4
- branching: int32 [128], P('leaf'), may hold values from 1 to 8, as said below
- sibling: int32 [64, 2], P('leaf'), may hold values from 0 to 1, each once within a row
- node_block: bfloat16 [512, 128, 512], P('blk', 'leaf'), may hold values from -6 to 6
- na_rows: bfloat16 [262144, 512], P(('leaf', 'blk')), may hold values from -2 to 2
- na_weight: bfloat16 [262144], P(('leaf', 'blk')), may hold values from 0.25 to 4
- na_route: int32 [262144, 1], P(('leaf', 'blk')), may hold values from 0 to 127; in each aligned block of 512 rows (0 to 511, 512 to 1023, ...) at most 6 rows name the same one
Outputs:
- node_schur: float32 [512, 128, 512], P('blk', 'leaf')
- merged: float32 [512, 128, 512], P('blk', 'leaf')
The draws below stay inside these ranges and needn't reach their ends.
Inputs may be any that keep to these rules, and one draw needn't show every extreme that they name: `branching`: some node has exactly 8 children. `sibling`: each row is a permutation. `na_route`: within the rows of one device, no node is named by more than 6 rows, a bound that some block reaches.
All inputs are finite; a program needn't handle non-finite values.
Results may differ from the reference program's by a relative error of at most 0.0012.
Values may be sent and summed in bfloat16 or wider, within the bound.
A program may use at most 64 MiB of HBM per device.

```python
import math
import jax
import jax.numpy as jnp
import numpy as np
from jax import lax

S = 512
KL = 512
MAXB = 8
NODE_DEV = 2
NA_DEV = 512
SUBTREES = 64
NODES = 128
NA_ROWS = 262144
CAP = 6
N_BLK = 8


def draw_branching(key, part):
    first_key = jax.random.fold_in(key, 11)
    second_key = jax.random.fold_in(key, 12)
    third_key = jax.random.fold_in(key, 13)
    fourth_key = jax.random.fold_in(key, 14)
    level = jax.random.randint(first_key, (SUBTREES,), 1, MAXB + 1)
    forced = jax.random.randint(second_key, (), 0, SUBTREES)
    level = jnp.where(jnp.arange(SUBTREES) == forced, MAXB, level)
    counts = jax.random.randint(third_key, (SUBTREES, NODE_DEV), 1, level[:, None] + 1)
    picked = jax.random.randint(fourth_key, (SUBTREES,), 0, NODE_DEV)
    counts = jnp.where(jnp.arange(NODE_DEV)[None, :] == picked[:, None], level[:, None], counts)
    return counts.reshape(-1).astype(jnp.int32)


def shard_levels(own_key, extent, split, low, top_value):
    def one(axis_at, blocks):
        draws = jax.random.uniform(jax.random.fold_in(jax.random.fold_in(own_key, 6), axis_at), (blocks,), jnp.float32, low / len(split), top_value / len(split))
        return jnp.repeat(jnp.exp(draws), extent[axis_at] // blocks).reshape((-1,) + (1,) * (len(extent) - axis_at - 1))

    factor_of = one(*split[0])
    for cut in split[1:]:
        factor_of = factor_of * one(*cut)
    return factor_of


def routed_block(key, own, number, rows, number_of, top, bound, slope):
    ranking = jax.random.permutation(key, number_of)
    packed, ordinary = shares(number_of, rows * top, bound, slope, True), shares(number_of, rows * top, bound, slope, False)
    places = jnp.arange(number_of)

    def named(tallies, rotation):
        used = int((tallies > 0).sum())
        fixed = max(1, used // 4)
        shifted = fixed + (places - fixed + rotation * (used - fixed)) % max(1, number_of - fixed)
        return jnp.zeros((number_of,), jnp.int32).at[ranking[jnp.where(places < fixed, places, shifted)]].set(jnp.asarray(tallies, jnp.int32))

    tallies = jnp.where(number % 4 == 0, named(packed, number // 4), named(ordinary, number - number // 4 - 1))
    mixed = jax.random.permutation(jax.random.fold_in(own, 3), number_of)
    donor, receiver = mixed[0:number_of // 2 * 2:2], mixed[1:number_of // 2 * 2:2]
    margin = jnp.minimum(tallies[donor] - 1, bound - tallies[receiver]) // 2
    margin = jnp.where((donor == ranking[0]) | (receiver == ranking[0]) | (tallies[receiver] == 0), 0, jnp.maximum(margin, 0))
    shifted = jax.random.randint(jax.random.fold_in(own, 4), (number_of // 2,), 0, 1 << 20) % (margin + 1)
    tallies = tallies.at[donor].add(-shifted).at[receiver].add(shifted)
    members = jnp.searchsorted(jnp.cumsum(tallies), jnp.arange(rows * top), side="right").astype(jnp.int32)
    grid = members.reshape(top, rows).T
    grid = grid[jax.random.permutation(jax.random.fold_in(own, 1), rows)]
    rotation = jax.random.randint(jax.random.fold_in(own, 2), (rows, 1), 0, top)
    return jnp.take_along_axis(grid, (jnp.arange(top)[None, :] + rotation) % top, axis=1)


def shares(number_of, total, limit, skew, full):
    weights = [(1 << 20) // math.isqrt(grade ** skew) + 1 for grade in range(1, number_of + 1)]
    largest = limit if full else min(limit, max(-(-total // number_of), total * weights[0] // sum(weights)))
    least = 1 if total - largest >= number_of - 1 else 0
    given, surplus = [largest] + [least] * (number_of - 1), total - largest - least * (number_of - 1)
    while surplus > 0:
        free = [i for i in range(1, number_of) if given[i] < largest] or [i for i in range(1, number_of) if given[i] < limit]
        mass, budget = sum([weights[i] for i in free]), surplus
        for i in free:
            extra = min(limit - given[i], max(1, budget * weights[i] // mass), surplus)
            given[i] = given[i] + extra
            surplus = surplus - extra
    return np.array(given)


def bell_draw(stream_key, shape, scale, bound, pieces=(), kind=jnp.bfloat16):
    array = scale * jax.random.normal(stream_key, shape, jnp.float32)
    if pieces:
        array = array * shard_levels(stream_key, shape, pieces, -0.22, 0.18)
    return jnp.clip(array, -bound, bound).astype(kind)


def setup_inputs(seed: int = 0) -> dict:
    streams_of = jax.random.split(jax.random.key(seed), 9)
    leaf_rows = bell_draw(streams_of[0], (NODES, MAXB, KL, S), ((MAXB * KL) ** -0.25), 2.0, ((0, 64), (2, 8)))
    leaf_weight = jnp.clip(jnp.exp(math.log(4.0) - 2.7725887 * jax.random.uniform(streams_of[1], (NODES, MAXB, KL), jnp.float32) ** shard_levels(streams_of[1], (NODES, MAXB, KL), ((0, 64), (2, 8)), -0.2, 0.2)), 0.25, 4.0).astype(jnp.bfloat16)
    branching = draw_branching(jax.random.fold_in(streams_of[8], 71), 0)
    sibling = jax.vmap(lambda own: jax.random.permutation(own, NODE_DEV))(jax.random.split(streams_of[3], SUBTREES)).reshape((SUBTREES, NODE_DEV)).astype(jnp.int32)
    node_block = bell_draw(streams_of[4], (S, NODES, S), 1.0, 6.0, ((0, 8), (1, 64)))
    na_rows = bell_draw(streams_of[5], (NA_ROWS, S), ((NA_DEV * N_BLK // NODE_DEV) ** -0.25), 2.0, ((0, 512),))
    na_weight = jnp.clip(jnp.exp(math.log(4.0) - 2.7725887 * jax.random.uniform(streams_of[6], (NA_ROWS,), jnp.float32) ** shard_levels(streams_of[6], (NA_ROWS,), ((0, 512),), -0.2, 0.2)), 0.25, 4.0).astype(jnp.bfloat16)
    na_route_keys = jax.random.split(jax.random.fold_in(streams_of[7], 1), NA_ROWS // NA_DEV)
    na_route_turns = jax.random.permutation(jax.random.fold_in(streams_of[7], 3), NA_ROWS // NA_DEV)
    na_route = jax.vmap(lambda own, number: routed_block(jax.random.fold_in(streams_of[7], 2), own, number, NA_DEV, NODES, 1, CAP, 2))(na_route_keys, na_route_turns).reshape((NA_ROWS, 1))
    return {"leaf_rows": leaf_rows, "leaf_weight": leaf_weight, "branching": branching, "sibling": sibling, "node_block": node_block, "na_rows": na_rows, "na_weight": na_weight, "na_route": na_route}


def bucket_rows(route, rows, weight, total_nodes, capacity):
    count = route.shape[0]
    order = jnp.argsort(route, stable=True)
    sorted_route = route[order].astype(jnp.int32)
    first = jnp.searchsorted(sorted_route, sorted_route, side="left").astype(jnp.int32)
    position = jnp.arange(count, dtype=jnp.int32) - first
    slot = sorted_route * capacity + position
    width = rows.shape[1]
    filled = jnp.zeros((total_nodes * capacity, width), rows.dtype).at[slot].set(rows[order])
    weights = jnp.zeros((total_nodes * capacity,), weight.dtype).at[slot].set(weight[order])
    return filled, weights


def reference(leaf_rows, leaf_weight, branching, sibling, node_block, na_rows, na_weight, na_route):
    live = (jnp.arange(MAXB, dtype=jnp.int32)[None, :] < branching[:, None]).astype(jnp.float32)

    def one_node(items):
        rows, weight, alive = items
        scaled = (rows.astype(jnp.float32) * (weight.astype(jnp.float32) * alive[:, None])[..., None]).astype(jnp.bfloat16)
        return jnp.dot(scaled.reshape(-1, S).T, rows.reshape(-1, S), preferred_element_type=jnp.float32)

    leaf_sum = lax.map(one_node, (leaf_rows, leaf_weight, live))
    blocks = NA_ROWS // NA_DEV
    block_rows = na_rows.reshape(blocks, NA_DEV, S)
    block_weight = na_weight.reshape(blocks, NA_DEV)
    block_route = na_route.reshape(blocks, NA_DEV)

    def add_block(carry, items):
        rows, weight, route = items
        filled, weights = bucket_rows(route, rows, weight, NODES, CAP)
        scaled = (filled.astype(jnp.float32) * weights.astype(jnp.float32)[:, None]).astype(jnp.bfloat16)
        scaled = scaled.reshape(NODES, CAP, S).astype(jnp.float32)
        plain = filled.reshape(NODES, CAP, S).astype(jnp.float32)
        term = jnp.einsum("ncs,nct->nst", scaled, plain, precision=lax.Precision.HIGHEST)
        return carry + term, None

    na_sum, _ = lax.scan(add_block, jnp.zeros((NODES, S, S), jnp.float32), (block_rows, block_weight, block_route))
    node_schur = node_block.astype(jnp.float32) + jnp.transpose(leaf_sum + na_sum, (1, 0, 2))
    index = jnp.arange(NODES, dtype=jnp.int32)
    subtree = index // NODE_DEV
    within = index % NODE_DEV
    partner = jnp.bitwise_xor(subtree, 1) * NODE_DEV + sibling[subtree, within]
    merged = node_schur + jnp.take(node_schur, partner.astype(jnp.int32), axis=1)
    return node_schur, merged
```

```python
import functools

import jax
import jax.numpy as jnp
from jax import lax
from jax.experimental import pallas as pl
from jax.experimental.pallas import tpu as pltpu
from jax.sharding import PartitionSpec as P

MESH = pl.DeviceIdType.MESH
F32 = jnp.float32
BF16 = jnp.bfloat16
WIRE = jnp.float32
ROWS_Y, ROWS_Z, CORES = 4, 8, 2
SIZE_X, SIZE_YH = 4, 2
CAP = 6
GROUP = 8


def outer_sum(scaled, plain):
    return lax.dot_general(
        scaled, plain, (((0,), (0,)), ((), ())), preferred_element_type=F32
    )


def kernel(
    branching,
    sibling,
    leaf_rows,
    leaf_weight,
    node_block,
    na_rows,
    na_weight,
    na_route,
    schur_out,
    merged_out,
    packed,
    packed_w,
    got,
    got_w,
    part,
    half,
    xs,
    xr,
    ys,
    yr,
    pr,
    a_send,
    a_recv,
    w_send,
    w_recv,
    x_send,
    x_recv,
    y_send,
    y_recv,
    p_send,
    p_recv,
    own_sem,
):
    leaves = ROWS_Y * ROWS_Z * CORES
    me = lax.axis_index("leaf")
    blk = lax.axis_index("blk")
    core, at_z, at_y = me % CORES, (me // CORES) % ROWS_Z, me // (CORES * ROWS_Z)
    at_x, at_yh = blk % SIZE_X, blk // SIZE_X
    state = na_rows.shape[1]
    count = na_rows.shape[0]
    lanes = 128
    block = state // (SIZE_X * SIZE_YH)

    def peer(k):
        mixed = (k * 27) % leaves
        to_core = (core + mixed % CORES) % CORES
        to_z = (at_z + (mixed // CORES) % ROWS_Z) % ROWS_Z
        to_y = (at_y + mixed // (CORES * ROWS_Z)) % ROWS_Y
        return (to_y * ROWS_Z + to_z) * CORES + to_core

    def x_peer(dx):
        return at_yh * SIZE_X + (at_x + dx) % SIZE_X

    yh_peer = (1 - at_yh) * SIZE_X + at_x
    partner = (me // CORES) * CORES + (1 - core)

    barrier = pltpu.get_barrier_semaphore()

    def greet(k, carry):
        pl.semaphore_signal(barrier, inc=1, device_id={"leaf": peer(k)}, device_id_type=MESH)
        return carry

    lax.fori_loop(1, leaves, greet, 0)
    for dx in range(1, SIZE_X):
        pl.semaphore_signal(barrier, inc=1, device_id={"blk": x_peer(dx)}, device_id_type=MESH)
    pl.semaphore_signal(barrier, inc=1, device_id={"blk": yh_peer}, device_id_type=MESH)

    route = na_route[...]
    route_f = route.astype(F32)
    at_diag = lax.broadcasted_iota(jnp.int32, (lanes, lanes), 0) == lax.broadcasted_iota(
        jnp.int32, (lanes, lanes), 1
    )
    place = jnp.zeros((1, count), F32)
    for b in range(count // lanes):
        own = route_f[:, b * lanes : (b + 1) * lanes]
        column = jnp.sum(jnp.where(at_diag, own, 0.0), axis=1, keepdims=True)
        earlier = lax.broadcasted_iota(jnp.int32, (lanes, count), 0) + b * lanes
        later = lax.broadcasted_iota(jnp.int32, (lanes, count), 1)
        same = (column == route_f) & (earlier < later)
        place = place + jnp.sum(jnp.where(same, 1.0, 0.0), axis=0, keepdims=True)
    slot = (route % 2) * (leaves * GROUP) + (route // 2) * GROUP + place.astype(jnp.int32)
    weight = na_weight[...].astype(F32)

    span = 128
    spans = leaves * GROUP // span
    subs = span // GROUP
    rank = lax.broadcasted_iota(jnp.int32, (span, lanes), 0) % GROUP
    lane = lax.broadcasted_iota(jnp.int32, (span, lanes), 1)

    def bucket(q):
        def one(i, carry):
            first = q * (leaves * GROUP) + i * span
            index = lax.broadcasted_iota(jnp.int32, (span, count), 0) + first
            hit = index == slot
            pick = jnp.where(hit, 1.0, 0.0).astype(BF16)
            filled = jnp.dot(pick, na_rows[...], preferred_element_type=F32)
            tail = filled[:, 3 * lanes :]
            at = pl.ds(i * subs, subs)
            for c in range(3):
                moved = pltpu.roll(tail, CAP - 2 * c, 0)
                tile = jnp.where(rank < CAP, filled[:, c * lanes : (c + 1) * lanes], moved)
                packed[q, at, c] = tile.reshape(subs, GROUP, lanes).astype(BF16)
            slot_w = jnp.sum(jnp.where(hit, weight, 0.0), axis=1, keepdims=True)
            spread = jnp.where(rank == lane, slot_w, 0.0).reshape(subs, GROUP, lanes)
            packed_w[q, at] = jnp.sum(spread, axis=1, keepdims=True)
            return carry

        lax.fori_loop(0, spans, one, 0)

    for q in range(2):
        bucket(q)

    pl.semaphore_wait(barrier, leaves - 1 + SIZE_X)

    for q in range(2):

        def send(k, carry):
            to = peer(k)
            pltpu.make_async_remote_copy(
                packed.at[q, to], got.at[q, me], a_send.at[q], a_recv.at[q],
                device_id={"leaf": to}, device_id_type=MESH,
            ).start()
            pltpu.make_async_remote_copy(
                packed_w.at[q, to], got_w.at[q, me], w_send.at[q], w_recv.at[q],
                device_id={"leaf": to}, device_id_type=MESH,
            ).start()
            return carry

        lax.fori_loop(1, leaves, send, 0)
    keep = []
    for q in range(2):
        keep.append(pltpu.make_async_copy(packed.at[q, me], got.at[q, me], own_sem.at[0, q]))
        keep.append(pltpu.make_async_copy(packed_w.at[q, me], got_w.at[q, me], own_sem.at[1, q]))
    for copy in keep:
        copy.start()

    children, rows_leaf = leaf_rows.shape[1], leaf_rows.shape[2]
    eye = lax.broadcasted_iota(jnp.int32, (rows_leaf, rows_leaf), 0) == lax.broadcasted_iota(
        jnp.int32, (rows_leaf, rows_leaf), 1
    )
    for q in range(2):
        scaled = []
        for b in range(children):
            w = leaf_weight[q, b : b + 1, :].astype(F32)
            w = jnp.sum(jnp.where(eye, w, 0.0), axis=1, keepdims=True)
            alive = (b < branching[q]).astype(F32)
            scaled.append((leaf_rows[q, b].astype(F32) * (w * alive)).astype(BF16))
        both = jnp.concatenate(scaled, axis=0)
        total = outer_sum(both, leaf_rows[q].reshape(children * rows_leaf, state))
        part[q] = total.reshape(SIZE_YH, SIZE_X, block, state)

    def rows_of(q):
        for copy in keep[2 * q : 2 * q + 2]:
            copy.wait()
        some = pl.ds(0, leaves - 1)
        pltpu.make_async_remote_copy(
            packed.at[q, some], got.at[q, some], a_send.at[q], a_recv.at[q],
            device_id={"leaf": partner}, device_id_type=MESH,
        ).wait_recv()
        pltpu.make_async_remote_copy(
            packed_w.at[q, some], got_w.at[q, some], w_send.at[q], w_recv.at[q],
            device_id={"leaf": partner}, device_id_type=MESH,
        ).wait_recv()
        total = leaves * GROUP
        r = lax.broadcasted_iota(jnp.int32, (total, lanes), 0) % GROUP
        tiles = [got[q, :, c].astype(F32).reshape(total, lanes) for c in range(3)]
        tail = jnp.zeros((total, lanes), F32)
        for c in range(3):
            moved = pltpu.roll(tiles[c], total - (CAP - 2 * c), 0)
            tail = jnp.where((r // 2) == c, moved, tail)
        r3 = lax.broadcasted_iota(jnp.int32, (leaves, GROUP, lanes), 1)
        l3 = lax.broadcasted_iota(jnp.int32, (leaves, GROUP, lanes), 2)
        w = jnp.where((r3 == l3) & (r3 < CAP), got_w[q], 0.0)
        w = jnp.sum(w, axis=2, keepdims=True).reshape(total, 1)
        plain = [t.astype(BF16) for t in tiles + [tail]]
        scaled = [(t * w).astype(BF16) for t in tiles + [tail]]
        return jnp.concatenate(scaled, axis=1), jnp.concatenate(plain, axis=1)

    def x_copy(q, dx):
        to = (at_x + dx) % SIZE_X
        return pltpu.make_async_remote_copy(
            xs.at[q, :, to], xr.at[q, dx - 1], x_send.at[q, dx - 1], x_recv.at[q, dx - 1],
            device_id={"blk": x_peer(dx)}, device_id_type=MESH,
        )

    def y_copy(q):
        return pltpu.make_async_remote_copy(
            ys.at[q], yr.at[q], y_send.at[q], y_recv.at[q],
            device_id={"blk": yh_peer}, device_id_type=MESH,
        )

    def p_copy(q):
        return pltpu.make_async_remote_copy(
            schur_out.at[q], pr.at[q], p_send.at[q], p_recv.at[q],
            device_id={"leaf": partner}, device_id_type=MESH,
        )

    def reduce_x(q):
        scaled, plain = rows_of(q)
        total = part[q] + outer_sum(scaled, plain).reshape(SIZE_YH, SIZE_X, block, state)
        part[q] = total
        xs[q] = total.astype(WIRE)
        for dx in (2, 1, 3):
            x_copy(q, dx).start()

    def reduce_y(q):
        for dx in (1, 3, 2):
            x_copy(q, dx).wait_recv()
        away = part[q, 1 - at_yh, at_x]
        for dx in range(SIZE_X - 1):
            away = away + xr[q, dx, 1 - at_yh].astype(F32)
        ys[q] = away.astype(WIRE)
        y_copy(q).start()
        mine = part[q, at_yh, at_x]
        for dx in range(SIZE_X - 1):
            mine = mine + xr[q, dx, at_yh].astype(F32)
        half[q] = mine + node_block[:, q, :].astype(F32)

    def finish(q):
        y_copy(q).wait_recv()
        schur_out[q] = half[q] + yr[q].astype(F32)
        p_copy(q).start()

    reduce_x(0)
    reduce_y(0)
    reduce_x(1)
    reduce_y(1)
    finish(0)
    finish(1)
    for q in range(2):
        p_copy(q).wait_recv()
    for q in range(2):
        choice = jnp.full((block, state), sibling[0, q], jnp.int32)
        merged_out[q] = schur_out[q] + jnp.where(choice == 0, pr[0], pr[1])

    some = pl.ds(0, leaves - 1)
    for q in range(2):
        pltpu.make_async_remote_copy(
            packed.at[q, some], got.at[q, some], a_send.at[q], a_recv.at[q],
            device_id={"leaf": partner}, device_id_type=MESH,
        ).wait_send()
        pltpu.make_async_remote_copy(
            packed_w.at[q, some], got_w.at[q, some], w_send.at[q], w_recv.at[q],
            device_id={"leaf": partner}, device_id_type=MESH,
        ).wait_send()
        for dx in range(1, SIZE_X):
            x_copy(q, dx).wait_send()
        y_copy(q).wait_send()
        p_copy(q).wait_send()


def shards(leaf_rows, leaf_weight, branching, sibling, node_block, na_rows, na_weight, na_route):
    leaves = ROWS_Y * ROWS_Z * CORES
    count, state = na_rows.shape
    block = state // (SIZE_X * SIZE_YH)
    vmem = pl.BlockSpec(memory_space=pltpu.VMEM)
    smem = pl.BlockSpec(memory_space=pltpu.SMEM)
    dma = pltpu.SemaphoreType.DMA
    schur, merged = pl.pallas_call(
        kernel,
        out_shape=[jax.ShapeDtypeStruct((2, block, state), F32)] * 2,
        in_specs=[smem, smem] + [vmem] * 6,
        out_specs=[vmem, vmem],
        scratch_shapes=[
            pltpu.VMEM((2, leaves, 3, GROUP, 128), BF16),
            pltpu.VMEM((2, leaves, 1, 128), F32),
            pltpu.VMEM((2, leaves, 3, GROUP, 128), BF16),
            pltpu.VMEM((2, leaves, 1, 128), F32),
            pltpu.VMEM((2, SIZE_YH, SIZE_X, block, state), F32),
            pltpu.VMEM((2, block, state), F32),
            pltpu.VMEM((2, SIZE_YH, SIZE_X, block, state), WIRE),
            pltpu.VMEM((2, SIZE_X - 1, SIZE_YH, block, state), WIRE),
            pltpu.VMEM((2, block, state), WIRE),
            pltpu.VMEM((2, block, state), WIRE),
            pltpu.VMEM((2, block, state), F32),
            dma((2,)),
            dma((2,)),
            dma((2,)),
            dma((2,)),
            dma((2, SIZE_X - 1)),
            dma((2, SIZE_X - 1)),
            dma((2,)),
            dma((2,)),
            dma((2,)),
            dma((2,)),
            dma((2, 2)),
        ],
        compiler_params=pltpu.CompilerParams(
            collective_id=0, has_side_effects=True, vmem_limit_bytes=60 << 20
        ),
        name="schur_pass",
    )(
        branching,
        sibling,
        leaf_rows,
        leaf_weight,
        node_block,
        na_rows,
        na_weight.reshape(1, count),
        na_route.reshape(1, count),
    )
    return jnp.transpose(schur, (1, 0, 2)), jnp.transpose(merged, (1, 0, 2))


def solution(mesh):
    return jax.shard_map(
        shards,
        mesh=mesh,
        in_specs=(
            P("leaf", None, "blk", None),
            P("leaf", None, "blk"),
            P("leaf"),
            P("leaf", None),
            P("blk", "leaf", None),
            P(("leaf", "blk"), None),
            P(("leaf", "blk")),
            P(("leaf", "blk"), None),
        ),
        out_specs=(P("blk", "leaf", None), P("blk", "leaf", None)),
        check_vma=False,
    )
```

```python
import functools

import jax
import jax.numpy as jnp
from jax import lax
from jax.experimental import pallas as pl
from jax.experimental.pallas import tpu as pltpu
from jax.sharding import PartitionSpec as P

MESH = pl.DeviceIdType.MESH
F32 = jnp.float32
BF16 = jnp.bfloat16
WIRE = jnp.int16
TOP = 32000.0
ROWS_Y, ROWS_Z, CORES = 4, 8, 2
SIZE_X, SIZE_YH = 4, 2
CAP = 6
GROUP = 8


def column_of(row, height):
    eye = lax.broadcasted_iota(jnp.int32, (height, row.shape[1]), 0) == lax.broadcasted_iota(
        jnp.int32, (height, row.shape[1]), 1
    )
    return jnp.sum(jnp.where(eye, row, 0.0), axis=1, keepdims=True)


def row_of(column):
    eye = lax.broadcasted_iota(jnp.int32, (column.shape[0], 128), 0) == lax.broadcasted_iota(
        jnp.int32, (column.shape[0], 128), 1
    )
    return jnp.sum(jnp.where(eye, column, 0.0), axis=0, keepdims=True)


def to_wire(values):
    peak = jnp.max(jnp.abs(values), axis=1, keepdims=True)
    peak = jnp.maximum(peak, 1e-30)
    return jnp.round(values * (TOP / peak)).astype(jnp.int32).astype(WIRE), peak * (1.0 / TOP)


def from_wire(values, unit_row):
    return values.astype(jnp.int32).astype(F32) * column_of(unit_row, values.shape[0])


def outer_sum(scaled, plain):
    return lax.dot_general(
        scaled, plain, (((0,), (0,)), ((), ())), preferred_element_type=F32
    )


def kernel(
    branching,
    sibling,
    leaf_rows,
    leaf_weight,
    node_block,
    na_rows,
    na_weight,
    na_route,
    schur_out,
    merged_out,
    packed,
    packed_w,
    got,
    got_w,
    part,
    half,
    xs,
    xs_unit,
    xr,
    xr_unit,
    ys,
    ys_unit,
    yr,
    yr_unit,
    pr,
    a_send,
    a_recv,
    w_send,
    w_recv,
    x_send,
    x_recv,
    xu_send,
    xu_recv,
    y_send,
    y_recv,
    yu_send,
    yu_recv,
    p_send,
    p_recv,
    own_sem,
):
    leaves = ROWS_Y * ROWS_Z * CORES
    me = lax.axis_index("leaf")
    blk = lax.axis_index("blk")
    core, at_z, at_y = me % CORES, (me // CORES) % ROWS_Z, me // (CORES * ROWS_Z)
    at_x, at_yh = blk % SIZE_X, blk // SIZE_X
    state = na_rows.shape[1]
    count = na_rows.shape[0]
    lanes = 128
    block = state // (SIZE_X * SIZE_YH)

    chips = ROWS_Y * ROWS_Z

    def chip_at(j):
        far = (j * 13) % chips
        return ((at_y + far // ROWS_Z) % ROWS_Y) * ROWS_Z + (at_z + far) % ROWS_Z

    def x_peer(dx):
        return at_yh * SIZE_X + (at_x + dx) % SIZE_X

    yh_peer = (1 - at_yh) * SIZE_X + at_x
    partner = (me // CORES) * CORES + (1 - core)

    barrier = pltpu.get_barrier_semaphore()

    def greet(j, carry):
        to = chip_at(j) * CORES
        for c in range(CORES):
            pl.semaphore_signal(barrier, inc=1, device_id={"leaf": to + c}, device_id_type=MESH)
        return carry

    lax.fori_loop(1, chips, greet, 0)
    pl.semaphore_signal(barrier, inc=1, device_id={"leaf": partner}, device_id_type=MESH)
    for dx in range(1, SIZE_X):
        pl.semaphore_signal(barrier, inc=1, device_id={"blk": x_peer(dx)}, device_id_type=MESH)
    pl.semaphore_signal(barrier, inc=1, device_id={"blk": yh_peer}, device_id_type=MESH)

    route = na_route[...]
    route_f = route.astype(F32)
    at_diag = lax.broadcasted_iota(jnp.int32, (lanes, lanes), 0) == lax.broadcasted_iota(
        jnp.int32, (lanes, lanes), 1
    )
    place = jnp.zeros((1, count), F32)
    for b in range(count // lanes):
        own = route_f[:, b * lanes : (b + 1) * lanes]
        column = jnp.sum(jnp.where(at_diag, own, 0.0), axis=1, keepdims=True)
        earlier = lax.broadcasted_iota(jnp.int32, (lanes, count), 0) + b * lanes
        later = lax.broadcasted_iota(jnp.int32, (lanes, count), 1)
        same = (column == route_f) & (earlier < later)
        place = place + jnp.sum(jnp.where(same, 1.0, 0.0), axis=0, keepdims=True)
    slot = (route % 2) * (leaves * GROUP) + (route // 2) * GROUP + place.astype(jnp.int32)
    weight = na_weight[...].astype(F32).reshape(1, count)

    span = 128
    spans = leaves * GROUP // span
    subs = span // GROUP
    rank = lax.broadcasted_iota(jnp.int32, (span, lanes), 0) % GROUP
    lane = lax.broadcasted_iota(jnp.int32, (span, lanes), 1)

    def bucket(q):
        def one(i, carry):
            first = q * (leaves * GROUP) + i * span
            index = lax.broadcasted_iota(jnp.int32, (span, count), 0) + first
            hit = index == slot
            pick = jnp.where(hit, 1.0, 0.0).astype(BF16)
            filled = jnp.dot(pick, na_rows[...], preferred_element_type=F32)
            tail = filled[:, 3 * lanes :]
            at = pl.ds(i * subs, subs)
            for c in range(3):
                moved = pltpu.roll(tail, CAP - 2 * c, 0)
                tile = jnp.where(rank < CAP, filled[:, c * lanes : (c + 1) * lanes], moved)
                packed[q, at, c] = tile.reshape(subs, GROUP, lanes).astype(BF16)
            slot_w = jnp.sum(jnp.where(hit, weight, 0.0), axis=1, keepdims=True)
            spread = jnp.where(rank + q * GROUP == lane, slot_w, 0.0).reshape(subs, GROUP, lanes)
            spread = jnp.sum(spread, axis=1, keepdims=True)
            packed_w[at] = spread if q == 0 else packed_w[at] + spread
            return carry

        lax.fori_loop(0, spans, one, 0)

    for q in range(2):
        bucket(q)

    pl.semaphore_wait(barrier, leaves - 1 + SIZE_X)

    def w_copy(to):
        return pltpu.make_async_remote_copy(
            packed_w.at[to], got_w.at[me], w_send, w_recv,
            device_id={"leaf": to}, device_id_type=MESH,
        )

    def a_copy(q, to):
        return pltpu.make_async_remote_copy(
            packed.at[q, to], got.at[q, me], a_send.at[q], a_recv.at[q],
            device_id={"leaf": to}, device_id_type=MESH,
        )

    w_copy(partner).start()
    for q in range(2):
        a_copy(q, partner).start()
    for q in range(2):
        for c in range(CORES):

            def send(j, carry):
                to = chip_at(j) * CORES + c
                if q == 0:
                    w_copy(to).start()
                a_copy(q, to).start()
                return carry

            lax.fori_loop(1, chips, send, 0)

    some = pl.ds(0, leaves - 1)

    def all_rows(q):
        return pltpu.make_async_remote_copy(
            packed.at[q, some], got.at[q, some], a_send.at[q], a_recv.at[q],
            device_id={"leaf": partner}, device_id_type=MESH,
        )

    def all_weights():
        return pltpu.make_async_remote_copy(
            packed_w.at[some], got_w.at[some], w_send, w_recv,
            device_id={"leaf": partner}, device_id_type=MESH,
        )

    keep = []
    for q in range(2):
        keep.append(pltpu.make_async_copy(packed.at[q, me], got.at[q, me], own_sem.at[0, q]))
    keep.append(pltpu.make_async_copy(packed_w.at[me], got_w.at[me], own_sem.at[1, 0]))
    for copy in keep:
        copy.start()

    children, rows_leaf = leaf_rows.shape[1], leaf_rows.shape[2]
    eye = lax.broadcasted_iota(jnp.int32, (rows_leaf, rows_leaf), 0) == lax.broadcasted_iota(
        jnp.int32, (rows_leaf, rows_leaf), 1
    )
    for q in range(2):
        scaled = []
        for b in range(children):
            w = leaf_weight[q, b : b + 1, :].astype(F32)
            w = jnp.sum(jnp.where(eye, w, 0.0), axis=1, keepdims=True)
            alive = (b < branching[q]).astype(F32)
            scaled.append((leaf_rows[q, b].astype(F32) * (w * alive)).astype(BF16))
        both = jnp.concatenate(scaled, axis=0)
        total = outer_sum(both, leaf_rows[q].reshape(children * rows_leaf, state))
        part[q] = total.reshape(SIZE_YH, SIZE_X, block, state)

    def rows_of(q):
        keep[q].wait()
        if q == 0:
            keep[2].wait()
            all_weights().wait_recv()
        all_rows(q).wait_recv()
        total = leaves * GROUP
        r = lax.broadcasted_iota(jnp.int32, (total, lanes), 0) % GROUP
        tiles = [got[q, :, c].astype(F32).reshape(total, lanes) for c in range(3)]
        tail = jnp.zeros((total, lanes), F32)
        for c in range(3):
            moved = pltpu.roll(tiles[c], total - (CAP - 2 * c), 0)
            tail = jnp.where((r // 2) == c, moved, tail)
        r3 = lax.broadcasted_iota(jnp.int32, (leaves, GROUP, lanes), 1)
        l3 = lax.broadcasted_iota(jnp.int32, (leaves, GROUP, lanes), 2)
        w = jnp.where((r3 + q * GROUP == l3) & (r3 < CAP), got_w[...], 0.0)
        w = jnp.sum(w, axis=2, keepdims=True).reshape(total, 1)
        plain = [t.astype(BF16) for t in tiles + [tail]]
        scaled = [(t * w).astype(BF16) for t in tiles + [tail]]
        return jnp.concatenate(scaled, axis=1), jnp.concatenate(plain, axis=1)

    def x_copies(q, dx):
        to = (at_x + dx) % SIZE_X
        ends = {"device_id": {"blk": x_peer(dx)}, "device_id_type": MESH}
        i = dx - 1
        unit = pltpu.make_async_remote_copy(
            xs_unit.at[q, :, to], xr_unit.at[q, i], xu_send.at[q, i], xu_recv.at[q, i], **ends
        )
        away, near = (
            pltpu.make_async_remote_copy(
                xs.at[q, yh, to], xr.at[q, i, yh], x_send.at[q, i, k], x_recv.at[q, i, k], **ends
            )
            for k, yh in enumerate((1 - at_yh, at_yh))
        )
        return unit, away, near

    def y_copies(q):
        ends = {"device_id": {"blk": yh_peer}, "device_id_type": MESH}
        return (
            pltpu.make_async_remote_copy(
                ys_unit.at[q], yr_unit.at[q], yu_send.at[q], yu_recv.at[q], **ends
            ),
            pltpu.make_async_remote_copy(
                ys.at[q], yr.at[q], y_send.at[q], y_recv.at[q], **ends
            ),
        )

    def p_copy(q):
        return pltpu.make_async_remote_copy(
            schur_out.at[q], pr.at[q], p_send.at[q], p_recv.at[q],
            device_id={"leaf": partner}, device_id_type=MESH,
        )

    def reduce_x(q):
        scaled, plain = rows_of(q)
        total = part[q] + outer_sum(scaled, plain).reshape(SIZE_YH, SIZE_X, block, state)
        part[q] = total
        for yh in range(SIZE_YH):
            for x in range(SIZE_X):
                xs[q, yh, x], unit = to_wire(total[yh, x])
                xs_unit[q, yh, x] = row_of(unit)
        order = [x_copies(q, dx) for dx in (2, 1, 3)]
        for k in range(3):
            for copies in order:
                copies[k].start()

    def sum_x(q, yh):
        total = part[q, yh, at_x]
        for i in range(SIZE_X - 1):
            total = total + from_wire(xr[q, i, yh], xr_unit[q, i, yh])
        return total

    def reduce_y(q):
        order = [x_copies(q, dx) for dx in (1, 3, 2)]
        for k in range(2):
            for copies in order:
                copies[k].wait_recv()
        ys[q], unit = to_wire(sum_x(q, 1 - at_yh))
        ys_unit[q] = row_of(unit)
        for copy in y_copies(q):
            copy.start()
        for copies in order:
            copies[2].wait_recv()
        half[q] = sum_x(q, at_yh) + node_block[:, q, :].astype(F32)

    def finish(q):
        for copy in y_copies(q):
            copy.wait_recv()
        schur_out[q] = half[q] + from_wire(yr[q], yr_unit[q])
        p_copy(q).start()

    reduce_x(0)
    reduce_y(0)
    reduce_x(1)
    reduce_y(1)
    finish(0)
    finish(1)
    for q in range(2):
        p_copy(q).wait_recv()
    for q in range(2):
        choice = jnp.full((block, state), sibling[0, q], jnp.int32)
        merged_out[q] = schur_out[q] + jnp.where(choice == 0, pr[0], pr[1])

    all_weights().wait_send()
    for q in range(2):
        all_rows(q).wait_send()
        for dx in range(1, SIZE_X):
            for copy in x_copies(q, dx):
                copy.wait_send()
        for copy in y_copies(q):
            copy.wait_send()
        p_copy(q).wait_send()


def arrange(schur, merged, schur_out, merged_out):
    for q in range(2):
        schur_out[:, q, :] = schur[q]
        merged_out[:, q, :] = merged[q]


def shards(leaf_rows, leaf_weight, branching, sibling, node_block, na_rows, na_weight, na_route):
    leaves = ROWS_Y * ROWS_Z * CORES
    count, state = na_rows.shape
    block = state // (SIZE_X * SIZE_YH)
    vmem = pl.BlockSpec(memory_space=pltpu.VMEM)
    smem = pl.BlockSpec(memory_space=pltpu.SMEM)
    dma = pltpu.SemaphoreType.DMA
    schur, merged = pl.pallas_call(
        kernel,
        out_shape=[jax.ShapeDtypeStruct((2, block, state), F32)] * 2,
        in_specs=[smem, smem] + [vmem] * 6,
        out_specs=[vmem, vmem],
        scratch_shapes=[
            pltpu.VMEM((2, leaves, 3, GROUP, 128), BF16),
            pltpu.VMEM((leaves, 1, 128), F32),
            pltpu.VMEM((2, leaves, 3, GROUP, 128), BF16),
            pltpu.VMEM((leaves, 1, 128), F32),
            pltpu.VMEM((2, SIZE_YH, SIZE_X, block, state), F32),
            pltpu.VMEM((2, block, state), F32),
            pltpu.VMEM((2, SIZE_YH, SIZE_X, block, state), WIRE),
            pltpu.VMEM((2, SIZE_YH, SIZE_X, 1, 128), F32),
            pltpu.VMEM((2, SIZE_X - 1, SIZE_YH, block, state), WIRE),
            pltpu.VMEM((2, SIZE_X - 1, SIZE_YH, 1, 128), F32),
            pltpu.VMEM((2, block, state), WIRE),
            pltpu.VMEM((2, 1, 128), F32),
            pltpu.VMEM((2, block, state), WIRE),
            pltpu.VMEM((2, 1, 128), F32),
            pltpu.VMEM((2, block, state), F32),
            dma((2,)),
            dma((2,)),
            dma(()),
            dma(()),
            dma((2, SIZE_X - 1, 2)),
            dma((2, SIZE_X - 1, 2)),
            dma((2, SIZE_X - 1)),
            dma((2, SIZE_X - 1)),
            dma((2,)),
            dma((2,)),
            dma((2,)),
            dma((2,)),
            dma((2,)),
            dma((2,)),
            dma((2, 2)),
        ],
        compiler_params=pltpu.CompilerParams(
            collective_id=0, has_side_effects=True, vmem_limit_bytes=60 << 20
        ),
        name="schur_pass",
    )(
        branching,
        sibling,
        leaf_rows,
        leaf_weight,
        node_block,
        na_rows,
        na_weight,
        na_route.reshape(1, count),
    )
    return pl.pallas_call(
        arrange,
        out_shape=[jax.ShapeDtypeStruct((block, 2, state), F32)] * 2,
        in_specs=[vmem, vmem],
        out_specs=[vmem, vmem],
        name="arrange",
    )(schur, merged)


def solution(mesh):
    return jax.shard_map(
        shards,
        mesh=mesh,
        in_specs=(
            P("leaf", None, "blk", None),
            P("leaf", None, "blk"),
            P("leaf"),
            P("leaf", None),
            P("blk", "leaf", None),
            P(("leaf", "blk"), None),
            P(("leaf", "blk")),
            P(("leaf", "blk"), None),
        ),
        out_specs=(P("blk", "leaf", None), P("blk", "leaf", None)),
        check_vma=False,
    )
```

```python
import functools

import jax
import jax.numpy as jnp
from jax import lax
from jax.experimental import pallas as pl
from jax.experimental.pallas import tpu as pltpu
from jax.sharding import PartitionSpec as P

MESH = pl.DeviceIdType.MESH
F32 = jnp.float32
BF16 = jnp.bfloat16
WIRE = jnp.int16
TOP = 32000.0
ROWS_Y, ROWS_Z, CORES = 4, 8, 2
SIZE_X, SIZE_YH = 4, 2
CAP = 6
GROUP = 8


def column_of(row, height):
    eye = lax.broadcasted_iota(jnp.int32, (height, row.shape[1]), 0) == lax.broadcasted_iota(
        jnp.int32, (height, row.shape[1]), 1
    )
    return jnp.sum(jnp.where(eye, row, 0.0), axis=1, keepdims=True)


def row_of(column):
    eye = lax.broadcasted_iota(jnp.int32, (column.shape[0], 128), 0) == lax.broadcasted_iota(
        jnp.int32, (column.shape[0], 128), 1
    )
    return jnp.sum(jnp.where(eye, column, 0.0), axis=0, keepdims=True)


def to_wire(values):
    peak = jnp.max(jnp.abs(values), axis=1, keepdims=True)
    peak = jnp.maximum(peak, 1e-30)
    return jnp.round(values * (TOP / peak)).astype(jnp.int32).astype(WIRE), peak * (1.0 / TOP)


def from_wire(values, unit_row):
    return values.astype(jnp.int32).astype(F32) * column_of(unit_row, values.shape[0])


def outer_sum(scaled, plain):
    return lax.dot_general(
        scaled, plain, (((0,), (0,)), ((), ())), preferred_element_type=F32
    )


def kernel(
    branching,
    sibling,
    leaf_rows_in,
    leaf_weight,
    node_block_in,
    na_rows_in,
    na_weight,
    na_route,
    schur_out,
    merged_out,
    leaf_rows,
    node_block,
    na_rows,
    packed,
    packed_w,
    got,
    got_w,
    part,
    half,
    xs,
    xs_unit,
    xr,
    xr_unit,
    ys,
    ys_unit,
    yr,
    yr_unit,
    pr,
    a_send,
    a_recv,
    w_send,
    w_recv,
    x_send,
    x_recv,
    xu_send,
    xu_recv,
    y_send,
    y_recv,
    yu_send,
    yu_recv,
    p_send,
    p_recv,
    own_sem,
    in_sem,
):
    leaves = ROWS_Y * ROWS_Z * CORES
    me = lax.axis_index("leaf")
    blk = lax.axis_index("blk")
    core, at_z, at_y = me % CORES, (me // CORES) % ROWS_Z, me // (CORES * ROWS_Z)
    at_x, at_yh = blk % SIZE_X, blk // SIZE_X
    state = na_rows.shape[1]
    count = na_rows.shape[0]
    lanes = 128
    block = state // (SIZE_X * SIZE_YH)

    chips = ROWS_Y * ROWS_Z

    def chip_at(j):
        a = j // ROWS_Y
        dz = ROWS_Z // 2 + (a // 2 + a % 2) * (1 - 2 * (a % 2))
        dy = ROWS_Y - 1 - j % ROWS_Y
        return ((at_y + dy) % ROWS_Y) * ROWS_Z + (at_z + dz) % ROWS_Z

    def x_peer(dx):
        return at_yh * SIZE_X + (at_x + dx) % SIZE_X

    yh_peer = (1 - at_yh) * SIZE_X + at_x
    partner = (me // CORES) * CORES + (1 - core)

    loads = [
        pltpu.make_async_copy(na_rows_in, na_rows, in_sem.at[0]),
        pltpu.make_async_copy(leaf_rows_in, leaf_rows, in_sem.at[1]),
        pltpu.make_async_copy(node_block_in, node_block, in_sem.at[2]),
    ]
    for load in loads:
        load.start()

    barrier = pltpu.get_barrier_semaphore()

    def greet(j, carry):
        to = chip_at(j) * CORES
        for c in range(CORES):
            pl.semaphore_signal(barrier, inc=1, device_id={"leaf": to + c}, device_id_type=MESH)
        return carry

    lax.fori_loop(0, chips - 1, greet, 0)
    pl.semaphore_signal(barrier, inc=1, device_id={"leaf": partner}, device_id_type=MESH)
    for dx in range(1, SIZE_X):
        pl.semaphore_signal(barrier, inc=1, device_id={"blk": x_peer(dx)}, device_id_type=MESH)
    pl.semaphore_signal(barrier, inc=1, device_id={"blk": yh_peer}, device_id_type=MESH)

    route = na_route[...]
    route_f = route.astype(F32)
    at_diag = lax.broadcasted_iota(jnp.int32, (lanes, lanes), 0) == lax.broadcasted_iota(
        jnp.int32, (lanes, lanes), 1
    )
    place = jnp.zeros((1, count), F32)
    for b in range(count // lanes):
        own = route_f[:, b * lanes : (b + 1) * lanes]
        column = jnp.sum(jnp.where(at_diag, own, 0.0), axis=1, keepdims=True)
        earlier = lax.broadcasted_iota(jnp.int32, (lanes, count), 0) + b * lanes
        later = lax.broadcasted_iota(jnp.int32, (lanes, count), 1)
        same = (column == route_f) & (earlier < later)
        place = place + jnp.sum(jnp.where(same, 1.0, 0.0), axis=0, keepdims=True)
    slot = (route % 2) * (leaves * GROUP) + (route // 2) * GROUP + place.astype(jnp.int32)
    weight = na_weight[...].astype(F32).reshape(1, count)

    span = 128
    spans = leaves * GROUP // span
    subs = span // GROUP
    rank = lax.broadcasted_iota(jnp.int32, (span, lanes), 0) % GROUP
    lane = lax.broadcasted_iota(jnp.int32, (span, lanes), 1)

    def bucket(q):
        def one(i, carry):
            first = q * (leaves * GROUP) + i * span
            index = lax.broadcasted_iota(jnp.int32, (span, count), 0) + first
            hit = index == slot
            pick = jnp.where(hit, 1.0, 0.0).astype(BF16)
            filled = jnp.dot(pick, na_rows[...], preferred_element_type=F32)
            tail = filled[:, 3 * lanes :]
            at = pl.ds(i * subs, subs)
            for c in range(3):
                moved = pltpu.roll(tail, CAP - 2 * c, 0)
                tile = jnp.where(rank < CAP, filled[:, c * lanes : (c + 1) * lanes], moved)
                packed[q, at, c] = tile.reshape(subs, GROUP, lanes).astype(BF16)
            slot_w = jnp.sum(jnp.where(hit, weight, 0.0), axis=1, keepdims=True)
            spread = jnp.where(rank + q * GROUP == lane, slot_w, 0.0).reshape(subs, GROUP, lanes)
            spread = jnp.sum(spread, axis=1, keepdims=True)
            packed_w[at] = spread if q == 0 else packed_w[at] + spread
            return carry

        lax.fori_loop(0, spans, one, 0)

    loads[0].wait()
    for q in range(2):
        bucket(q)

    pl.semaphore_wait(barrier, leaves - 1 + SIZE_X)

    def w_copy(to):
        return pltpu.make_async_remote_copy(
            packed_w.at[to], got_w.at[me], w_send, w_recv,
            device_id={"leaf": to}, device_id_type=MESH,
        )

    def a_copy(q, to):
        return pltpu.make_async_remote_copy(
            packed.at[q, to], got.at[q, me], a_send.at[q], a_recv.at[q],
            device_id={"leaf": to}, device_id_type=MESH,
        )

    w_copy(partner).start()
    for q in range(2):
        a_copy(q, partner).start()
    for q, c in ((0, 1), (0, 0), (1, 0), (1, 1)):

        def send(j, carry):
            to = chip_at(j) * CORES + c
            if q == 0:
                w_copy(to).start()
            a_copy(q, to).start()
            return carry

        lax.fori_loop(0, chips - 1, send, 0)

    some = pl.ds(0, leaves - 1)

    def all_rows(q):
        return pltpu.make_async_remote_copy(
            packed.at[q, some], got.at[q, some], a_send.at[q], a_recv.at[q],
            device_id={"leaf": partner}, device_id_type=MESH,
        )

    def all_weights():
        return pltpu.make_async_remote_copy(
            packed_w.at[some], got_w.at[some], w_send, w_recv,
            device_id={"leaf": partner}, device_id_type=MESH,
        )

    keep = []
    for q in range(2):
        keep.append(pltpu.make_async_copy(packed.at[q, me], got.at[q, me], own_sem.at[0, q]))
    keep.append(pltpu.make_async_copy(packed_w.at[me], got_w.at[me], own_sem.at[1, 0]))
    for copy in keep:
        copy.start()

    for load in loads[1:]:
        load.wait()

    children, rows_leaf = leaf_rows.shape[1], leaf_rows.shape[2]
    eye = lax.broadcasted_iota(jnp.int32, (rows_leaf, rows_leaf), 0) == lax.broadcasted_iota(
        jnp.int32, (rows_leaf, rows_leaf), 1
    )
    for q in range(2):
        scaled = []
        for b in range(children):
            w = leaf_weight[q, b : b + 1, :].astype(F32)
            w = jnp.sum(jnp.where(eye, w, 0.0), axis=1, keepdims=True)
            alive = (b < branching[q]).astype(F32)
            scaled.append((leaf_rows[q, b].astype(F32) * (w * alive)).astype(BF16))
        both = jnp.concatenate(scaled, axis=0)
        total = outer_sum(both, leaf_rows[q].reshape(children * rows_leaf, state))
        part[q] = total.reshape(SIZE_YH, SIZE_X, block, state)

    def rows_of(q):
        keep[q].wait()
        if q == 0:
            keep[2].wait()
            all_weights().wait_recv()
        all_rows(q).wait_recv()
        total = leaves * GROUP
        r = lax.broadcasted_iota(jnp.int32, (total, lanes), 0) % GROUP
        tiles = [got[q, :, c].astype(F32).reshape(total, lanes) for c in range(3)]
        tail = jnp.zeros((total, lanes), F32)
        for c in range(3):
            moved = pltpu.roll(tiles[c], total - (CAP - 2 * c), 0)
            tail = jnp.where((r // 2) == c, moved, tail)
        r3 = lax.broadcasted_iota(jnp.int32, (leaves, GROUP, lanes), 1)
        l3 = lax.broadcasted_iota(jnp.int32, (leaves, GROUP, lanes), 2)
        w = jnp.where((r3 + q * GROUP == l3) & (r3 < CAP), got_w[...], 0.0)
        w = jnp.sum(w, axis=2, keepdims=True).reshape(total, 1)
        plain = [t.astype(BF16) for t in tiles + [tail]]
        scaled = [(t * w).astype(BF16) for t in tiles + [tail]]
        return jnp.concatenate(scaled, axis=1), jnp.concatenate(plain, axis=1)

    def x_copies(q, dx):
        to = (at_x + dx) % SIZE_X
        ends = {"device_id": {"blk": x_peer(dx)}, "device_id_type": MESH}
        i = dx - 1
        unit = pltpu.make_async_remote_copy(
            xs_unit.at[q, :, to], xr_unit.at[q, i], xu_send.at[q, i], xu_recv.at[q, i], **ends
        )
        away, near = (
            pltpu.make_async_remote_copy(
                xs.at[q, yh, to], xr.at[q, i, yh], x_send.at[q, i, k], x_recv.at[q, i, k], **ends
            )
            for k, yh in enumerate((1 - at_yh, at_yh))
        )
        return unit, away, near

    def y_copies(q):
        ends = {"device_id": {"blk": yh_peer}, "device_id_type": MESH}
        return (
            pltpu.make_async_remote_copy(
                ys_unit.at[q], yr_unit.at[q], yu_send.at[q], yu_recv.at[q], **ends
            ),
            pltpu.make_async_remote_copy(
                ys.at[q], yr.at[q], y_send.at[q], y_recv.at[q], **ends
            ),
        )

    def p_copy(q):
        return pltpu.make_async_remote_copy(
            schur_out.at[q], pr.at[q], p_send.at[q], p_recv.at[q],
            device_id={"leaf": partner}, device_id_type=MESH,
        )

    def reduce_x(q):
        scaled, plain = rows_of(q)
        total = part[q] + outer_sum(scaled, plain).reshape(SIZE_YH, SIZE_X, block, state)
        part[q] = total
        for yh in range(SIZE_YH):
            for x in range(SIZE_X):
                xs[q, yh, x], unit = to_wire(total[yh, x])
                xs_unit[q, yh, x] = row_of(unit)
        order = [x_copies(q, dx) for dx in (2, 1, 3)]
        for k in range(3):
            for copies in order:
                copies[k].start()

    def sum_x(q, yh):
        total = part[q, yh, at_x]
        for i in range(SIZE_X - 1):
            total = total + from_wire(xr[q, i, yh], xr_unit[q, i, yh])
        return total

    def reduce_y(q):
        order = [x_copies(q, dx) for dx in (1, 3, 2)]
        for k in range(2):
            for copies in order:
                copies[k].wait_recv()
        ys[q], unit = to_wire(sum_x(q, 1 - at_yh))
        ys_unit[q] = row_of(unit)
        for copy in y_copies(q):
            copy.start()
        for copies in order:
            copies[2].wait_recv()
        half[q] = sum_x(q, at_yh) + node_block[:, q, :].astype(F32)

    def finish(q):
        for copy in y_copies(q):
            copy.wait_recv()
        schur_out[q] = half[q] + from_wire(yr[q], yr_unit[q])
        p_copy(q).start()

    reduce_x(0)
    reduce_x(1)
    reduce_y(0)
    reduce_y(1)
    finish(0)
    finish(1)
    for q in range(2):
        p_copy(q).wait_recv()
    for q in range(2):
        choice = jnp.full((block, state), sibling[0, q], jnp.int32)
        merged_out[q] = schur_out[q] + jnp.where(choice == 0, pr[0], pr[1])

    all_weights().wait_send()
    for q in range(2):
        all_rows(q).wait_send()
        for dx in range(1, SIZE_X):
            for copy in x_copies(q, dx):
                copy.wait_send()
        for copy in y_copies(q):
            copy.wait_send()
        p_copy(q).wait_send()


def arrange(schur, merged, schur_out, merged_out):
    for q in range(2):
        schur_out[:, q, :] = schur[q]
        merged_out[:, q, :] = merged[q]


def shards(leaf_rows, leaf_weight, branching, sibling, node_block, na_rows, na_weight, na_route):
    leaves = ROWS_Y * ROWS_Z * CORES
    count, state = na_rows.shape
    block = state // (SIZE_X * SIZE_YH)
    vmem = pl.BlockSpec(memory_space=pltpu.VMEM)
    smem = pl.BlockSpec(memory_space=pltpu.SMEM)
    hbm = pl.BlockSpec(memory_space=pl.ANY)
    dma = pltpu.SemaphoreType.DMA
    schur, merged = pl.pallas_call(
        kernel,
        out_shape=[pltpu.VMEM((2, block, state), F32)] * 2,
        in_specs=[smem, smem, hbm, vmem, hbm, hbm, vmem, vmem],
        out_specs=[vmem, vmem],
        scratch_shapes=[
            pltpu.VMEM(leaf_rows.shape, BF16),
            pltpu.VMEM(node_block.shape, BF16),
            pltpu.VMEM(na_rows.shape, BF16),
            pltpu.VMEM((2, leaves, 3, GROUP, 128), BF16),
            pltpu.VMEM((leaves, 1, 128), F32),
            pltpu.VMEM((2, leaves, 3, GROUP, 128), BF16),
            pltpu.VMEM((leaves, 1, 128), F32),
            pltpu.VMEM((2, SIZE_YH, SIZE_X, block, state), F32),
            pltpu.VMEM((2, block, state), F32),
            pltpu.VMEM((2, SIZE_YH, SIZE_X, block, state), WIRE),
            pltpu.VMEM((2, SIZE_YH, SIZE_X, 1, 128), F32),
            pltpu.VMEM((2, SIZE_X - 1, SIZE_YH, block, state), WIRE),
            pltpu.VMEM((2, SIZE_X - 1, SIZE_YH, 1, 128), F32),
            pltpu.VMEM((2, block, state), WIRE),
            pltpu.VMEM((2, 1, 128), F32),
            pltpu.VMEM((2, block, state), WIRE),
            pltpu.VMEM((2, 1, 128), F32),
            pltpu.VMEM((2, block, state), F32),
            dma((2,)),
            dma((2,)),
            dma(()),
            dma(()),
            dma((2, SIZE_X - 1, 2)),
            dma((2, SIZE_X - 1, 2)),
            dma((2, SIZE_X - 1)),
            dma((2, SIZE_X - 1)),
            dma((2,)),
            dma((2,)),
            dma((2,)),
            dma((2,)),
            dma((2,)),
            dma((2,)),
            dma((2, 2)),
            dma((3,)),
        ],
        compiler_params=pltpu.CompilerParams(
            collective_id=0, has_side_effects=True, vmem_limit_bytes=60 << 20
        ),
        name="schur_pass",
    )(
        branching,
        sibling,
        leaf_rows,
        leaf_weight,
        node_block,
        na_rows,
        na_weight,
        na_route.reshape(1, count),
    )
    return pl.pallas_call(
        arrange,
        out_shape=[jax.ShapeDtypeStruct((block, 2, state), F32)] * 2,
        in_specs=[vmem, vmem],
        out_specs=[vmem, vmem],
        name="arrange",
    )(
        pltpu.with_memory_space_constraint(schur, pltpu.VMEM),
        pltpu.with_memory_space_constraint(merged, pltpu.VMEM),
    )


def solution(mesh):
    return jax.shard_map(
        shards,
        mesh=mesh,
        in_specs=(
            P("leaf", None, "blk", None),
            P("leaf", None, "blk"),
            P("leaf"),
            P("leaf", None),
            P("blk", "leaf", None),
            P(("leaf", "blk"), None),
            P(("leaf", "blk")),
            P(("leaf", "blk"), None),
        ),
        out_specs=(P("blk", "leaf", None), P("blk", "leaf", None)),
        check_vma=False,
    )
```

```python
import functools

import jax
import jax.numpy as jnp
from jax import lax
from jax.experimental import pallas as pl
from jax.experimental.pallas import tpu as pltpu
from jax.sharding import PartitionSpec as P

MESH = pl.DeviceIdType.MESH
F32 = jnp.float32
BF16 = jnp.bfloat16
WIRE = jnp.int16
TOP = 32000.0
ROWS_Y, ROWS_Z, CORES = 4, 8, 2
SIZE_X, SIZE_YH = 4, 2
CAP = 6
GROUP = 8


def column_of(row, height):
    eye = lax.broadcasted_iota(jnp.int32, (height, row.shape[1]), 0) == lax.broadcasted_iota(
        jnp.int32, (height, row.shape[1]), 1
    )
    return jnp.sum(jnp.where(eye, row, 0.0), axis=1, keepdims=True)


def row_of(column):
    eye = lax.broadcasted_iota(jnp.int32, (column.shape[0], 128), 0) == lax.broadcasted_iota(
        jnp.int32, (column.shape[0], 128), 1
    )
    return jnp.sum(jnp.where(eye, column, 0.0), axis=0, keepdims=True)


def to_wire(values):
    peak = jnp.max(jnp.abs(values), axis=1, keepdims=True)
    peak = jnp.maximum(peak, 1e-30)
    return jnp.round(values * (TOP / peak)).astype(jnp.int32).astype(WIRE), peak * (1.0 / TOP)


def from_wire(values, unit_row):
    return values.astype(jnp.int32).astype(F32) * column_of(unit_row, values.shape[0])


def outer_sum(scaled, plain):
    return lax.dot_general(
        scaled, plain, (((0,), (0,)), ((), ())), preferred_element_type=F32
    )


def kernel(
    branching_in,
    sibling_in,
    leaf_rows_in,
    leaf_weight_in,
    node_block_in,
    na_rows_in,
    na_weight_in,
    na_route_in,
    schur_out,
    merged_out,
    branching,
    sibling,
    leaf_rows,
    leaf_weight,
    node_block,
    na_rows,
    na_weight,
    na_route,
    packed,
    packed_w,
    got,
    got_w,
    part,
    half,
    xs,
    xs_unit,
    xr,
    xr_unit,
    ys,
    ys_unit,
    yr,
    yr_unit,
    pr,
    a_send,
    a_recv,
    w_send,
    w_recv,
    x_send,
    x_recv,
    xu_send,
    xu_recv,
    y_send,
    y_recv,
    yu_send,
    yu_recv,
    p_send,
    p_recv,
    own_sem,
    in_sem,
):
    leaves = ROWS_Y * ROWS_Z * CORES
    me = lax.axis_index("leaf")
    blk = lax.axis_index("blk")
    core, at_z, at_y = me % CORES, (me // CORES) % ROWS_Z, me // (CORES * ROWS_Z)
    at_x, at_yh = blk % SIZE_X, blk // SIZE_X
    state = na_rows.shape[1]
    count = na_rows.shape[0]
    lanes = 128
    block = state // (SIZE_X * SIZE_YH)

    chips = ROWS_Y * ROWS_Z

    def chip_at(j):
        a = j // ROWS_Y
        dz = ROWS_Z // 2 + (a // 2 + a % 2) * (1 - 2 * (a % 2))
        dy = ROWS_Y - 1 - j % ROWS_Y
        return ((at_y + dy) % ROWS_Y) * ROWS_Z + (at_z + dz) % ROWS_Z

    def x_peer(dx):
        return at_yh * SIZE_X + (at_x + dx) % SIZE_X

    yh_peer = (1 - at_yh) * SIZE_X + at_x
    partner = (me // CORES) * CORES + (1 - core)

    loads = [
        pltpu.make_async_copy(src, dst, in_sem.at[i])
        for i, (src, dst) in enumerate(
            (
                (na_route_in, na_route),
                (na_weight_in, na_weight),
                (na_rows_in, na_rows),
                (leaf_weight_in, leaf_weight),
                (leaf_rows_in, leaf_rows),
                (node_block_in, node_block),
                (branching_in, branching),
                (sibling_in, sibling),
            )
        )
    ]
    for load in loads:
        load.start()

    barrier = pltpu.get_barrier_semaphore()

    def greet(j, carry):
        to = chip_at(j) * CORES
        for c in range(CORES):
            pl.semaphore_signal(barrier, inc=1, device_id={"leaf": to + c}, device_id_type=MESH)
        return carry

    lax.fori_loop(0, chips - 1, greet, 0)
    pl.semaphore_signal(barrier, inc=1, device_id={"leaf": partner}, device_id_type=MESH)
    for dx in range(1, SIZE_X):
        pl.semaphore_signal(barrier, inc=1, device_id={"blk": x_peer(dx)}, device_id_type=MESH)
    pl.semaphore_signal(barrier, inc=1, device_id={"blk": yh_peer}, device_id_type=MESH)

    for load in loads[:3]:
        load.wait()

    route = na_route[...]
    route_f = route.astype(F32)
    at_diag = lax.broadcasted_iota(jnp.int32, (lanes, lanes), 0) == lax.broadcasted_iota(
        jnp.int32, (lanes, lanes), 1
    )
    place = jnp.zeros((1, count), F32)
    for b in range(count // lanes):
        own = route_f[:, b * lanes : (b + 1) * lanes]
        column = jnp.sum(jnp.where(at_diag, own, 0.0), axis=1, keepdims=True)
        earlier = lax.broadcasted_iota(jnp.int32, (lanes, count), 0) + b * lanes
        later = lax.broadcasted_iota(jnp.int32, (lanes, count), 1)
        same = (column == route_f) & (earlier < later)
        place = place + jnp.sum(jnp.where(same, 1.0, 0.0), axis=0, keepdims=True)
    slot = (route % 2) * (leaves * GROUP) + (route // 2) * GROUP + place.astype(jnp.int32)
    weight = na_weight[...].astype(F32).reshape(1, count)

    span = 128
    spans = leaves * GROUP // span
    subs = span // GROUP
    rank = lax.broadcasted_iota(jnp.int32, (span, lanes), 0) % GROUP
    lane = lax.broadcasted_iota(jnp.int32, (span, lanes), 1)

    def bucket(q):
        def one(i, carry):
            first = q * (leaves * GROUP) + i * span
            index = lax.broadcasted_iota(jnp.int32, (span, count), 0) + first
            hit = index == slot
            pick = jnp.where(hit, 1.0, 0.0).astype(BF16)
            filled = jnp.dot(pick, na_rows[...], preferred_element_type=F32)
            tail = filled[:, 3 * lanes :]
            at = pl.ds(i * subs, subs)
            for c in range(3):
                moved = pltpu.roll(tail, CAP - 2 * c, 0)
                tile = jnp.where(rank < CAP, filled[:, c * lanes : (c + 1) * lanes], moved)
                packed[q, at, c] = tile.reshape(subs, GROUP, lanes).astype(BF16)
            slot_w = jnp.sum(jnp.where(hit, weight, 0.0), axis=1, keepdims=True)
            spread = jnp.where(rank + q * GROUP == lane, slot_w, 0.0).reshape(subs, GROUP, lanes)
            spread = jnp.sum(spread, axis=1, keepdims=True)
            packed_w[at] = spread if q == 0 else packed_w[at] + spread
            return carry

        lax.fori_loop(0, spans, one, 0)

    for q in range(2):
        bucket(q)

    pl.semaphore_wait(barrier, leaves - 1 + SIZE_X)

    def w_copy(to):
        return pltpu.make_async_remote_copy(
            packed_w.at[to], got_w.at[me], w_send, w_recv,
            device_id={"leaf": to}, device_id_type=MESH,
        )

    def a_copy(q, to):
        return pltpu.make_async_remote_copy(
            packed.at[q, to], got.at[q, me], a_send.at[q], a_recv.at[q],
            device_id={"leaf": to}, device_id_type=MESH,
        )

    w_copy(partner).start()
    for q in range(2):
        a_copy(q, partner).start()
    def send_unit(q, c):

        def send(j, carry):
            to = chip_at(j) * CORES + c
            if q == 0:
                w_copy(to).start()
            a_copy(q, to).start()
            return carry

        lax.fori_loop(0, chips - 1, send, 0)

    for q, c in ((0, 1), (0, 0)):
        send_unit(q, c)
    for load in loads[3:]:
        load.wait()

    children, rows_leaf = leaf_rows.shape[1], leaf_rows.shape[2]
    eye = lax.broadcasted_iota(jnp.int32, (rows_leaf, rows_leaf), 0) == lax.broadcasted_iota(
        jnp.int32, (rows_leaf, rows_leaf), 1
    )
    for q in range(2):
        scaled = []
        for b in range(children):
            w = leaf_weight[q, b : b + 1, :].astype(F32)
            w = jnp.sum(jnp.where(eye, w, 0.0), axis=1, keepdims=True)
            alive = (b < branching[q]).astype(F32)
            scaled.append((leaf_rows[q, b].astype(F32) * (w * alive)).astype(BF16))
        both = jnp.concatenate(scaled, axis=0)
        total = outer_sum(both, leaf_rows[q].reshape(children * rows_leaf, state))
        part[q] = total.reshape(SIZE_YH, SIZE_X, block, state)

    for q, c in ((1, 0), (1, 1)):
        send_unit(q, c)
    some = pl.ds(0, leaves - 1)

    def all_rows(q):
        return pltpu.make_async_remote_copy(
            packed.at[q, some], got.at[q, some], a_send.at[q], a_recv.at[q],
            device_id={"leaf": partner}, device_id_type=MESH,
        )

    def all_weights():
        return pltpu.make_async_remote_copy(
            packed_w.at[some], got_w.at[some], w_send, w_recv,
            device_id={"leaf": partner}, device_id_type=MESH,
        )

    keep = []
    for q in range(2):
        keep.append(pltpu.make_async_copy(packed.at[q, me], got.at[q, me], own_sem.at[0, q]))
    keep.append(pltpu.make_async_copy(packed_w.at[me], got_w.at[me], own_sem.at[1, 0]))
    for copy in keep:
        copy.start()

    def rows_of(q):
        keep[q].wait()
        if q == 0:
            keep[2].wait()
            all_weights().wait_recv()
        all_rows(q).wait_recv()
        total = leaves * GROUP
        r = lax.broadcasted_iota(jnp.int32, (total, lanes), 0) % GROUP
        tiles = [got[q, :, c].astype(F32).reshape(total, lanes) for c in range(3)]
        tail = jnp.zeros((total, lanes), F32)
        for c in range(3):
            moved = pltpu.roll(tiles[c], total - (CAP - 2 * c), 0)
            tail = jnp.where((r // 2) == c, moved, tail)
        r3 = lax.broadcasted_iota(jnp.int32, (leaves, GROUP, lanes), 1)
        l3 = lax.broadcasted_iota(jnp.int32, (leaves, GROUP, lanes), 2)
        w = jnp.where((r3 + q * GROUP == l3) & (r3 < CAP), got_w[...], 0.0)
        w = jnp.sum(w, axis=2, keepdims=True).reshape(total, 1)
        plain = [t.astype(BF16) for t in tiles + [tail]]
        scaled = [(t * w).astype(BF16) for t in tiles + [tail]]
        return jnp.concatenate(scaled, axis=1), jnp.concatenate(plain, axis=1)

    def x_copies(q, dx):
        to = (at_x + dx) % SIZE_X
        ends = {"device_id": {"blk": x_peer(dx)}, "device_id_type": MESH}
        i = dx - 1
        unit = pltpu.make_async_remote_copy(
            xs_unit.at[q, :, to], xr_unit.at[q, i], xu_send.at[q, i], xu_recv.at[q, i], **ends
        )
        away, near = (
            pltpu.make_async_remote_copy(
                xs.at[q, yh, to], xr.at[q, i, yh], x_send.at[q, i, k], x_recv.at[q, i, k], **ends
            )
            for k, yh in enumerate((1 - at_yh, at_yh))
        )
        return unit, away, near

    def y_copies(q):
        ends = {"device_id": {"blk": yh_peer}, "device_id_type": MESH}
        return (
            pltpu.make_async_remote_copy(
                ys_unit.at[q], yr_unit.at[q], yu_send.at[q], yu_recv.at[q], **ends
            ),
            pltpu.make_async_remote_copy(
                ys.at[q], yr.at[q], y_send.at[q], y_recv.at[q], **ends
            ),
        )

    def p_copy(q):
        return pltpu.make_async_remote_copy(
            schur_out.at[q], pr.at[q], p_send.at[q], p_recv.at[q],
            device_id={"leaf": partner}, device_id_type=MESH,
        )

    def reduce_x(q):
        scaled, plain = rows_of(q)
        total = part[q] + outer_sum(scaled, plain).reshape(SIZE_YH, SIZE_X, block, state)
        part[q] = total
        for yh in range(SIZE_YH):
            for x in range(SIZE_X):
                xs[q, yh, x], unit = to_wire(total[yh, x])
                xs_unit[q, yh, x] = row_of(unit)
        order = [x_copies(q, dx) for dx in (2, 1, 3)]
        for k in range(3):
            for copies in order:
                copies[k].start()

    def sum_x(q, yh):
        total = part[q, yh, at_x]
        for i in range(SIZE_X - 1):
            total = total + from_wire(xr[q, i, yh], xr_unit[q, i, yh])
        return total

    def reduce_y(q):
        order = [x_copies(q, dx) for dx in (1, 3, 2)]
        for k in range(2):
            for copies in order:
                copies[k].wait_recv()
        ys[q], unit = to_wire(sum_x(q, 1 - at_yh))
        ys_unit[q] = row_of(unit)
        for copy in y_copies(q):
            copy.start()
        for copies in order:
            copies[2].wait_recv()
        half[q] = sum_x(q, at_yh) + node_block[:, q, :].astype(F32)

    def finish(q):
        for copy in y_copies(q):
            copy.wait_recv()
        schur_out[q] = half[q] + from_wire(yr[q], yr_unit[q])
        p_copy(q).start()

    reduce_x(0)
    reduce_x(1)
    reduce_y(0)
    reduce_y(1)
    finish(0)
    finish(1)
    for q in range(2):
        p_copy(q).wait_recv()
    for q in range(2):
        choice = jnp.full((block, state), sibling[0, q], jnp.int32)
        merged_out[q] = schur_out[q] + jnp.where(choice == 0, pr[0], pr[1])

    all_weights().wait_send()
    for q in range(2):
        all_rows(q).wait_send()
        for dx in range(1, SIZE_X):
            for copy in x_copies(q, dx):
                copy.wait_send()
        for copy in y_copies(q):
            copy.wait_send()
        p_copy(q).wait_send()


def arrange(schur, merged, schur_out, merged_out):
    for q in range(2):
        schur_out[:, q, :] = schur[q]
        merged_out[:, q, :] = merged[q]


def shards(leaf_rows, leaf_weight, branching, sibling, node_block, na_rows, na_weight, na_route):
    leaves = ROWS_Y * ROWS_Z * CORES
    count, state = na_rows.shape
    block = state // (SIZE_X * SIZE_YH)
    vmem = pl.BlockSpec(memory_space=pltpu.VMEM)
    hbm = pl.BlockSpec(memory_space=pl.ANY)
    dma = pltpu.SemaphoreType.DMA
    schur, merged = pl.pallas_call(
        kernel,
        out_shape=[pltpu.VMEM((2, block, state), F32)] * 2,
        in_specs=[hbm] * 8,
        out_specs=[vmem, vmem],
        scratch_shapes=[
            pltpu.SMEM(branching.shape, jnp.int32),
            pltpu.SMEM(sibling.shape, jnp.int32),
            pltpu.VMEM(leaf_rows.shape, BF16),
            pltpu.VMEM(leaf_weight.shape, BF16),
            pltpu.VMEM(node_block.shape, BF16),
            pltpu.VMEM(na_rows.shape, BF16),
            pltpu.VMEM(na_weight.shape, BF16),
            pltpu.VMEM((1, count), jnp.int32),
            pltpu.VMEM((2, leaves, 3, GROUP, 128), BF16),
            pltpu.VMEM((leaves, 1, 128), F32),
            pltpu.VMEM((2, leaves, 3, GROUP, 128), BF16),
            pltpu.VMEM((leaves, 1, 128), F32),
            pltpu.VMEM((2, SIZE_YH, SIZE_X, block, state), F32),
            pltpu.VMEM((2, block, state), F32),
            pltpu.VMEM((2, SIZE_YH, SIZE_X, block, state), WIRE),
            pltpu.VMEM((2, SIZE_YH, SIZE_X, 1, 128), F32),
            pltpu.VMEM((2, SIZE_X - 1, SIZE_YH, block, state), WIRE),
            pltpu.VMEM((2, SIZE_X - 1, SIZE_YH, 1, 128), F32),
            pltpu.VMEM((2, block, state), WIRE),
            pltpu.VMEM((2, 1, 128), F32),
            pltpu.VMEM((2, block, state), WIRE),
            pltpu.VMEM((2, 1, 128), F32),
            pltpu.VMEM((2, block, state), F32),
            dma((2,)),
            dma((2,)),
            dma(()),
            dma(()),
            dma((2, SIZE_X - 1, 2)),
            dma((2, SIZE_X - 1, 2)),
            dma((2, SIZE_X - 1)),
            dma((2, SIZE_X - 1)),
            dma((2,)),
            dma((2,)),
            dma((2,)),
            dma((2,)),
            dma((2,)),
            dma((2,)),
            dma((2, 2)),
            dma((8,)),
        ],
        compiler_params=pltpu.CompilerParams(
            collective_id=0, has_side_effects=True, vmem_limit_bytes=60 << 20
        ),
        name="schur_pass",
    )(
        branching,
        sibling,
        leaf_rows,
        leaf_weight,
        node_block,
        na_rows,
        na_weight,
        na_route.reshape(1, count),
    )
    return pl.pallas_call(
        arrange,
        out_shape=[jax.ShapeDtypeStruct((block, 2, state), F32)] * 2,
        in_specs=[vmem, vmem],
        out_specs=[vmem, vmem],
        name="arrange",
    )(
        pltpu.with_memory_space_constraint(schur, pltpu.VMEM),
        pltpu.with_memory_space_constraint(merged, pltpu.VMEM),
    )


def solution(mesh):
    return jax.shard_map(
        shards,
        mesh=mesh,
        in_specs=(
            P("leaf", None, "blk", None),
            P("leaf", None, "blk"),
            P("leaf"),
            P("leaf", None),
            P("blk", "leaf", None),
            P(("leaf", "blk"), None),
            P(("leaf", "blk")),
            P(("leaf", "blk"), None),
        ),
        out_specs=(P("blk", "leaf", None), P("blk", "leaf", None)),
        check_vma=False,
    )
```

```python
import functools

import jax
import jax.numpy as jnp
from jax import lax
from jax.experimental import pallas as pl
from jax.experimental.pallas import tpu as pltpu
from jax.sharding import PartitionSpec as P

MESH = pl.DeviceIdType.MESH
F32 = jnp.float32
BF16 = jnp.bfloat16
WIRE = jnp.int16
TOP = 32000.0
ROWS_Y, ROWS_Z, CORES = 4, 8, 2
SIZE_X, SIZE_YH = 4, 2
CAP = 6
GROUP = 8


def column_of(row, height):
    eye = lax.broadcasted_iota(jnp.int32, (height, row.shape[1]), 0) == lax.broadcasted_iota(
        jnp.int32, (height, row.shape[1]), 1
    )
    return jnp.sum(jnp.where(eye, row, 0.0), axis=1, keepdims=True)


def row_of(column):
    eye = lax.broadcasted_iota(jnp.int32, (column.shape[0], 128), 0) == lax.broadcasted_iota(
        jnp.int32, (column.shape[0], 128), 1
    )
    return jnp.sum(jnp.where(eye, column, 0.0), axis=0, keepdims=True)


def to_wire(values):
    peak = jnp.max(jnp.abs(values), axis=1, keepdims=True)
    peak = jnp.maximum(peak, 1e-30)
    return jnp.round(values * (TOP / peak)).astype(jnp.int32).astype(WIRE), peak * (1.0 / TOP)


def from_wire(values, unit_row):
    return values.astype(jnp.int32).astype(F32) * column_of(unit_row, values.shape[0])


def outer_sum(scaled, plain):
    return lax.dot_general(
        scaled, plain, (((0,), (0,)), ((), ())), preferred_element_type=F32
    )


def kernel(
    branching_in,
    sibling_in,
    leaf_rows_in,
    leaf_weight_in,
    node_block_in,
    na_rows_in,
    na_weight_in,
    na_route_in,
    schur_all,
    merged_all,
    branching,
    sibling,
    leaf_rows,
    leaf_weight,
    node_block,
    na_rows,
    na_weight,
    na_route,
    packed,
    packed_w,
    got,
    got_w,
    part,
    half,
    xs,
    xs_unit,
    xr,
    xr_unit,
    ys,
    ys_unit,
    yr,
    yr_unit,
    pr,
    a_send,
    a_recv,
    w_send,
    w_recv,
    x_send,
    x_recv,
    xu_send,
    xu_recv,
    y_send,
    y_recv,
    yu_send,
    yu_recv,
    p_send,
    p_recv,
    own_sem,
    in_sem,
    schur_out,
):
    leaves = ROWS_Y * ROWS_Z * CORES
    me = lax.axis_index("leaf")
    blk = lax.axis_index("blk")
    core, at_z, at_y = me % CORES, (me // CORES) % ROWS_Z, me // (CORES * ROWS_Z)
    at_x, at_yh = blk % SIZE_X, blk // SIZE_X
    state = na_rows.shape[1]
    count = na_rows.shape[0]
    lanes = 128
    block = state // (SIZE_X * SIZE_YH)

    chips = ROWS_Y * ROWS_Z

    def chip_at(j):
        a = j // ROWS_Y
        dz = ROWS_Z // 2 + (a // 2 + a % 2) * (1 - 2 * (a % 2))
        dy = ROWS_Y - 1 - j % ROWS_Y
        return ((at_y + dy) % ROWS_Y) * ROWS_Z + (at_z + dz) % ROWS_Z

    def x_peer(dx):
        return at_yh * SIZE_X + (at_x + dx) % SIZE_X

    yh_peer = (1 - at_yh) * SIZE_X + at_x
    partner = (me // CORES) * CORES + (1 - core)

    loads = [
        pltpu.make_async_copy(src, dst, in_sem.at[i])
        for i, (src, dst) in enumerate(
            (
                (na_route_in, na_route),
                (na_weight_in, na_weight),
                (na_rows_in, na_rows),
                (leaf_weight_in, leaf_weight),
                (leaf_rows_in, leaf_rows),
                (node_block_in, node_block),
                (branching_in, branching),
                (sibling_in, sibling),
            )
        )
    ]
    for load in loads:
        load.start()

    barrier = pltpu.get_barrier_semaphore()

    def greet(j, carry):
        to = chip_at(j) * CORES
        for c in range(CORES):
            pl.semaphore_signal(barrier, inc=1, device_id={"leaf": to + c}, device_id_type=MESH)
        return carry

    lax.fori_loop(0, chips - 1, greet, 0)
    pl.semaphore_signal(barrier, inc=1, device_id={"leaf": partner}, device_id_type=MESH)
    for dx in range(1, SIZE_X):
        pl.semaphore_signal(barrier, inc=1, device_id={"blk": x_peer(dx)}, device_id_type=MESH)
    pl.semaphore_signal(barrier, inc=1, device_id={"blk": yh_peer}, device_id_type=MESH)

    for load in loads[:3]:
        load.wait()

    route = na_route[...]
    route_f = route.astype(F32)
    at_diag = lax.broadcasted_iota(jnp.int32, (lanes, lanes), 0) == lax.broadcasted_iota(
        jnp.int32, (lanes, lanes), 1
    )
    place = jnp.zeros((1, count), F32)
    for b in range(count // lanes):
        own = route_f[:, b * lanes : (b + 1) * lanes]
        column = jnp.sum(jnp.where(at_diag, own, 0.0), axis=1, keepdims=True)
        earlier = lax.broadcasted_iota(jnp.int32, (lanes, count), 0) + b * lanes
        later = lax.broadcasted_iota(jnp.int32, (lanes, count), 1)
        same = (column == route_f) & (earlier < later)
        place = place + jnp.sum(jnp.where(same, 1.0, 0.0), axis=0, keepdims=True)
    slot = (route % 2) * (leaves * GROUP) + (route // 2) * GROUP + place.astype(jnp.int32)
    weight = na_weight[...].astype(F32).reshape(1, count)

    span = 128
    spans = leaves * GROUP // span
    subs = span // GROUP
    rank = lax.broadcasted_iota(jnp.int32, (span, lanes), 0) % GROUP
    lane = lax.broadcasted_iota(jnp.int32, (span, lanes), 1)

    def bucket(q):
        def one(i, carry):
            first = q * (leaves * GROUP) + i * span
            index = lax.broadcasted_iota(jnp.int32, (span, count), 0) + first
            hit = index == slot
            pick = jnp.where(hit, 1.0, 0.0).astype(BF16)
            filled = jnp.dot(pick, na_rows[...], preferred_element_type=F32)
            tail = filled[:, 3 * lanes :]
            at = pl.ds(i * subs, subs)
            for c in range(3):
                moved = pltpu.roll(tail, CAP - 2 * c, 0)
                tile = jnp.where(rank < CAP, filled[:, c * lanes : (c + 1) * lanes], moved)
                packed[q, at, c] = tile.reshape(subs, GROUP, lanes).astype(BF16)
            slot_w = jnp.sum(jnp.where(hit, weight, 0.0), axis=1, keepdims=True)
            spread = jnp.where(rank + q * GROUP == lane, slot_w, 0.0).reshape(subs, GROUP, lanes)
            spread = jnp.sum(spread, axis=1, keepdims=True)
            packed_w[at] = spread if q == 0 else packed_w[at] + spread
            return carry

        lax.fori_loop(0, spans, one, 0)

    for q in range(2):
        bucket(q)

    pl.semaphore_wait(barrier, leaves - 1 + SIZE_X)

    def w_copy(to):
        return pltpu.make_async_remote_copy(
            packed_w.at[to], got_w.at[me], w_send, w_recv,
            device_id={"leaf": to}, device_id_type=MESH,
        )

    def a_copy(q, to):
        return pltpu.make_async_remote_copy(
            packed.at[q, to], got.at[q, me], a_send.at[q], a_recv.at[q],
            device_id={"leaf": to}, device_id_type=MESH,
        )

    w_copy(partner).start()
    for q in range(2):
        a_copy(q, partner).start()
    def send_unit(q, c):

        def send(j, carry):
            to = chip_at(j) * CORES + c
            if q == 0:
                w_copy(to).start()
            a_copy(q, to).start()
            return carry

        lax.fori_loop(0, chips - 1, send, 0)

    for q, c in ((0, 1), (0, 0)):
        send_unit(q, c)
    for load in loads[3:]:
        load.wait()

    children, rows_leaf = leaf_rows.shape[1], leaf_rows.shape[2]
    eye = lax.broadcasted_iota(jnp.int32, (rows_leaf, rows_leaf), 0) == lax.broadcasted_iota(
        jnp.int32, (rows_leaf, rows_leaf), 1
    )
    for q in range(2):
        scaled = []
        for b in range(children):
            w = leaf_weight[q, b : b + 1, :].astype(F32)
            w = jnp.sum(jnp.where(eye, w, 0.0), axis=1, keepdims=True)
            alive = (b < branching[q]).astype(F32)
            scaled.append((leaf_rows[q, b].astype(F32) * (w * alive)).astype(BF16))
        both = jnp.concatenate(scaled, axis=0)
        total = outer_sum(both, leaf_rows[q].reshape(children * rows_leaf, state))
        part[q] = total.reshape(SIZE_YH, SIZE_X, block, state)

    for q, c in ((1, 0), (1, 1)):
        send_unit(q, c)
    some = pl.ds(0, leaves - 1)

    def all_rows(q):
        return pltpu.make_async_remote_copy(
            packed.at[q, some], got.at[q, some], a_send.at[q], a_recv.at[q],
            device_id={"leaf": partner}, device_id_type=MESH,
        )

    def all_weights():
        return pltpu.make_async_remote_copy(
            packed_w.at[some], got_w.at[some], w_send, w_recv,
            device_id={"leaf": partner}, device_id_type=MESH,
        )

    keep = []
    for q in range(2):
        keep.append(pltpu.make_async_copy(packed.at[q, me], got.at[q, me], own_sem.at[0, q]))
    keep.append(pltpu.make_async_copy(packed_w.at[me], got_w.at[me], own_sem.at[1, 0]))
    for copy in keep:
        copy.start()

    def rows_of(q):
        keep[q].wait()
        if q == 0:
            keep[2].wait()
            all_weights().wait_recv()
        all_rows(q).wait_recv()
        total = leaves * GROUP
        r = lax.broadcasted_iota(jnp.int32, (total, lanes), 0) % GROUP
        tiles = [got[q, :, c].astype(F32).reshape(total, lanes) for c in range(3)]
        tail = jnp.zeros((total, lanes), F32)
        for c in range(3):
            moved = pltpu.roll(tiles[c], total - (CAP - 2 * c), 0)
            tail = jnp.where((r // 2) == c, moved, tail)
        r3 = lax.broadcasted_iota(jnp.int32, (leaves, GROUP, lanes), 1)
        l3 = lax.broadcasted_iota(jnp.int32, (leaves, GROUP, lanes), 2)
        w = jnp.where((r3 + q * GROUP == l3) & (r3 < CAP), got_w[...], 0.0)
        w = jnp.sum(w, axis=2, keepdims=True).reshape(total, 1)
        plain = [t.astype(BF16) for t in tiles + [tail]]
        scaled = [(t * w).astype(BF16) for t in tiles + [tail]]
        return jnp.concatenate(scaled, axis=1), jnp.concatenate(plain, axis=1)

    def x_copies(q, dx):
        to = (at_x + dx) % SIZE_X
        ends = {"device_id": {"blk": x_peer(dx)}, "device_id_type": MESH}
        i = dx - 1
        unit = pltpu.make_async_remote_copy(
            xs_unit.at[q, :, to], xr_unit.at[q, i], xu_send.at[q, i], xu_recv.at[q, i], **ends
        )
        away, near = (
            pltpu.make_async_remote_copy(
                xs.at[q, yh, to], xr.at[q, i, yh], x_send.at[q, i, k], x_recv.at[q, i, k], **ends
            )
            for k, yh in enumerate((1 - at_yh, at_yh))
        )
        return unit, away, near

    def y_copies(q):
        ends = {"device_id": {"blk": yh_peer}, "device_id_type": MESH}
        return (
            pltpu.make_async_remote_copy(
                ys_unit.at[q], yr_unit.at[q], yu_send.at[q], yu_recv.at[q], **ends
            ),
            pltpu.make_async_remote_copy(
                ys.at[q], yr.at[q], y_send.at[q], y_recv.at[q], **ends
            ),
        )

    def p_copy(q):
        return pltpu.make_async_remote_copy(
            schur_out.at[q], pr.at[q], p_send.at[q], p_recv.at[q],
            device_id={"leaf": partner}, device_id_type=MESH,
        )

    def reduce_x(q):
        scaled, plain = rows_of(q)
        total = part[q] + outer_sum(scaled, plain).reshape(SIZE_YH, SIZE_X, block, state)
        part[q] = total
        for yh in range(SIZE_YH):
            for x in range(SIZE_X):
                xs[q, yh, x], unit = to_wire(total[yh, x])
                xs_unit[q, yh, x] = row_of(unit)
        order = [x_copies(q, dx) for dx in (2, 1, 3)]
        for k in range(3):
            for copies in order:
                copies[k].start()

    def sum_x(q, yh):
        total = part[q, yh, at_x]
        for i in range(SIZE_X - 1):
            total = total + from_wire(xr[q, i, yh], xr_unit[q, i, yh])
        return total

    def reduce_y(q):
        order = [x_copies(q, dx) for dx in (1, 3, 2)]
        for k in range(2):
            for copies in order:
                copies[k].wait_recv()
        ys[q], unit = to_wire(sum_x(q, 1 - at_yh))
        ys_unit[q] = row_of(unit)
        for copy in y_copies(q):
            copy.start()
        for copies in order:
            copies[2].wait_recv()
        half[q] = sum_x(q, at_yh) + node_block[:, q, :].astype(F32)

    def finish(q):
        for copy in y_copies(q):
            copy.wait_recv()
        schur_out[q] = half[q] + from_wire(yr[q], yr_unit[q])
        p_copy(q).start()
        schur_all[:, q, :] = schur_out[q]

    reduce_x(0)
    reduce_x(1)
    reduce_y(0)
    reduce_y(1)
    finish(0)
    finish(1)
    for q in range(2):
        p_copy(q).wait_recv()
    for q in range(2):
        choice = jnp.full((block, state), sibling[0, q], jnp.int32)
        merged_all[:, q, :] = schur_out[q] + jnp.where(choice == 0, pr[0], pr[1])

    all_weights().wait_send()
    for q in range(2):
        all_rows(q).wait_send()
        for dx in range(1, SIZE_X):
            for copy in x_copies(q, dx):
                copy.wait_send()
        for copy in y_copies(q):
            copy.wait_send()
        p_copy(q).wait_send()


def arrange(schur, merged, schur_out, merged_out, sem):
    copies = [
        pltpu.make_async_copy(schur, schur_out, sem.at[0]),
        pltpu.make_async_copy(merged, merged_out, sem.at[1]),
    ]
    for copy in copies:
        copy.start()
    for copy in copies:
        copy.wait()


def shards(leaf_rows, leaf_weight, branching, sibling, node_block, na_rows, na_weight, na_route):
    leaves = ROWS_Y * ROWS_Z * CORES
    count, state = na_rows.shape
    block = state // (SIZE_X * SIZE_YH)
    vmem = pl.BlockSpec(memory_space=pltpu.VMEM)
    hbm = pl.BlockSpec(memory_space=pl.ANY)
    dma = pltpu.SemaphoreType.DMA
    schur, merged = pl.pallas_call(
        kernel,
        out_shape=[pltpu.VMEM((block, 2, state), F32)] * 2,
        in_specs=[hbm] * 8,
        out_specs=[vmem, vmem],
        scratch_shapes=[
            pltpu.SMEM(branching.shape, jnp.int32),
            pltpu.SMEM(sibling.shape, jnp.int32),
            pltpu.VMEM(leaf_rows.shape, BF16),
            pltpu.VMEM(leaf_weight.shape, BF16),
            pltpu.VMEM(node_block.shape, BF16),
            pltpu.VMEM(na_rows.shape, BF16),
            pltpu.VMEM(na_weight.shape, BF16),
            pltpu.VMEM((1, count), jnp.int32),
            pltpu.VMEM((2, leaves, 3, GROUP, 128), BF16),
            pltpu.VMEM((leaves, 1, 128), F32),
            pltpu.VMEM((2, leaves, 3, GROUP, 128), BF16),
            pltpu.VMEM((leaves, 1, 128), F32),
            pltpu.VMEM((2, SIZE_YH, SIZE_X, block, state), F32),
            pltpu.VMEM((2, block, state), F32),
            pltpu.VMEM((2, SIZE_YH, SIZE_X, block, state), WIRE),
            pltpu.VMEM((2, SIZE_YH, SIZE_X, 1, 128), F32),
            pltpu.VMEM((2, SIZE_X - 1, SIZE_YH, block, state), WIRE),
            pltpu.VMEM((2, SIZE_X - 1, SIZE_YH, 1, 128), F32),
            pltpu.VMEM((2, block, state), WIRE),
            pltpu.VMEM((2, 1, 128), F32),
            pltpu.VMEM((2, block, state), WIRE),
            pltpu.VMEM((2, 1, 128), F32),
            pltpu.VMEM((2, block, state), F32),
            dma((2,)),
            dma((2,)),
            dma(()),
            dma(()),
            dma((2, SIZE_X - 1, 2)),
            dma((2, SIZE_X - 1, 2)),
            dma((2, SIZE_X - 1)),
            dma((2, SIZE_X - 1)),
            dma((2,)),
            dma((2,)),
            dma((2,)),
            dma((2,)),
            dma((2,)),
            dma((2,)),
            dma((2, 2)),
            dma((8,)),
            pltpu.VMEM((2, block, state), F32),
        ],
        compiler_params=pltpu.CompilerParams(
            collective_id=0, has_side_effects=True, vmem_limit_bytes=60 << 20
        ),
        name="schur_pass",
    )(
        branching,
        sibling,
        leaf_rows,
        leaf_weight,
        node_block,
        na_rows,
        na_weight,
        na_route.reshape(1, count),
    )
    return pl.pallas_call(
        arrange,
        out_shape=[jax.ShapeDtypeStruct((block, 2, state), F32)] * 2,
        in_specs=[vmem, vmem],
        out_specs=[hbm, hbm],
        scratch_shapes=[dma((2,))],
        name="arrange",
    )(
        pltpu.with_memory_space_constraint(schur, pltpu.VMEM),
        pltpu.with_memory_space_constraint(merged, pltpu.VMEM),
    )


def solution(mesh):
    return jax.shard_map(
        shards,
        mesh=mesh,
        in_specs=(
            P("leaf", None, "blk", None),
            P("leaf", None, "blk"),
            P("leaf"),
            P("leaf", None),
            P("blk", "leaf", None),
            P(("leaf", "blk"), None),
            P(("leaf", "blk")),
            P(("leaf", "blk"), None),
        ),
        out_specs=(P("blk", "leaf", None), P("blk", "leaf", None)),
        check_vma=False,
    )
```
